32 devices in a mesh: parts: 2 (over x), seq: 16 (over z, y, core).
Axes of the slice: x: 2, y: 2, z: 4, core: 2. Of those that a mesh axis runs over, the one named last changes fastest.
Arguments:
- conv_input: bfloat16 [32768, 2816], P(('parts', 'seq')), parts along dimension 0, may hold values from -6 to 6
- step_raw: bfloat16 [32768, 40], P(('parts', 'seq')), parts along dimension 0, may hold values from -4 to 4
- conv_weight: float32 [4, 2816], replicated, may hold values from -3 to 3
- conv_bias: float32 [2816], replicated, may hold values from -3 to 3
- step_bias: float32 [40], replicated, may hold values from -1 to 1
- decay_rate: float32 [40], replicated, may hold values from 1.8310547e-07 to 0.05, as said below
- norm_gain: float32 [2560], replicated, may hold values from 0.1 to 1.9
Outputs:
- layer_out: bfloat16 [32768, 2560], P(('parts', 'seq')), parts along dimension 0
The draws below stay inside these ranges and needn't reach their ends.
There are 2 independent parts, one for each index of `parts`. The reference program is written for one: setup_inputs(seed, part) draws one part's arguments, and reference() takes and returns one part's arrays. A program takes and returns all parts, laid end to end along the dimension named above; an argument that names none is the same for every part. Nothing has to cross between parts.
Inputs may be any that keep to these rules, and one draw needn't show every extreme that they name: `decay_rate`: positive decay rates, one per head.
All inputs are finite; a program needn't handle non-finite values.
Results may differ from the reference program's by a relative error of at most 0.0034.
Values may be sent and summed in bfloat16 or wider, within the bound.
A program may use at most 384 MiB of HBM per device.

```python
import math
import jax
import jax.numpy as jnp
from jax import lax

HEADS = 40
CONV = 4
GROUP = 256
INNER = 2560
CONV_DIM = 2816
TOKENS = 16384


def draw_decay_rate(key, part):
    lowest = math.log(0.003 / TOKENS)
    highest = math.log(0.05)
    spread = jax.random.uniform(jax.random.fold_in(key, 14), (HEADS,), jnp.float32, lowest, highest)
    return jnp.exp(spread).astype(jnp.float32)


def level_of(own_key, dims, cuts, smallest, largest):
    def one(dim, shards_of):
        draws = jax.random.uniform(jax.random.fold_in(jax.random.fold_in(own_key, 6), dim), (shards_of,), jnp.float32, smallest / len(cuts), largest / len(cuts))
        return jnp.repeat(jnp.exp(draws), dims[dim] // shards_of).reshape((-1,) + (1,) * (len(dims) - dim - 1))

    gain = one(*cuts[0])
    for cut in cuts[1:]:
        gain = gain * one(*cut)
    return gain


def bell_draw(key, dims, deviation, reach, cuts=(), held_as=jnp.bfloat16):
    gain = level_of(key, dims, cuts, -0.22, 0.18) if cuts else 1.0
    values = jax.random.normal(key, dims, jnp.float32) * deviation * gain
    return jnp.minimum(jnp.maximum(values, -reach), reach).astype(held_as)


def setup_inputs(seed: int = 0, part: int = 0) -> dict:
    arg_keys = jax.random.split(jax.random.key(seed), 8)
    part_splits = jax.random.split(jax.random.fold_in(arg_keys[7], part), 8)
    conv_input = bell_draw(part_splits[0], (TOKENS, CONV_DIM), 1.0, 6.0, ((0, 16),))
    step_raw = bell_draw(part_splits[1], (TOKENS, HEADS), 1.0, 4.0, ((0, 16),))
    conv_weight = bell_draw(arg_keys[2], (CONV, CONV_DIM), 0.5, 3.0, (), jnp.float32)
    conv_bias = bell_draw(arg_keys[3], (CONV_DIM,), 0.5, 3.0, (), jnp.float32)
    step_bias = jnp.clip(jax.random.uniform(arg_keys[4], (HEADS,), jnp.float32, -1.0, 1.0), -1.0, 1.0)
    decay_rate = draw_decay_rate(jax.random.fold_in(arg_keys[7], 71), part)
    norm_gain = jnp.clip(1.0 + 0.18 * jax.random.normal(arg_keys[6], (INNER,), jnp.float32), 0.1, 1.9)
    return {"conv_input": conv_input, "step_raw": step_raw, "conv_weight": conv_weight, "conv_bias": conv_bias, "step_bias": step_bias, "decay_rate": decay_rate, "norm_gain": norm_gain}


def conv_mix(padded, conv_weight, conv_bias, row_count):
    total = jnp.zeros((row_count, padded.shape[1]), jnp.float32) + conv_bias
    for offset in range(conv_weight.shape[0]):
        total = total + padded[offset:offset + row_count].astype(jnp.float32) * conv_weight[offset]
    return jax.nn.silu(total).astype(jnp.bfloat16)

def block_parts(values, inputs_b, inputs_c, step_sizes, log_decay):
    cumulative = jnp.cumsum(log_decay, axis=0)
    scores = jnp.dot(inputs_c, inputs_b.T, preferred_element_type=jnp.float32)
    span_rows = log_decay.shape[0]
    causal = jnp.tril(jnp.ones((span_rows, span_rows), dtype=bool))
    gap_table = cumulative.T[:, :, None] - cumulative.T[:, None, :]
    decay = jnp.where(causal[None], jnp.exp(jnp.where(causal[None], gap_table, 0.0)), 0.0)
    mixing = (scores[None] * decay * step_sizes.T[:, None, :]).astype(jnp.bfloat16)
    mixing = lax.optimization_barrier(mixing)
    within = jnp.einsum('hts,shp->thp', mixing.astype(jnp.float32), values.astype(jnp.float32))
    weights = jnp.exp(cumulative[-1][None, :] - cumulative) * step_sizes
    scaled = (weights[:, :, None] * values.astype(jnp.float32)).astype(jnp.bfloat16)
    scaled = lax.optimization_barrier(scaled)
    update = jnp.einsum('shp,sn->hpn', scaled.astype(jnp.float32), inputs_b.astype(jnp.float32))
    return (cumulative, within, update)

def finish(result, norm_gain):
    flat = result.reshape(result.shape[0], -1)
    scale = lax.rsqrt(lax.optimization_barrier(jnp.mean(flat * flat, axis=-1, keepdims=True)) + 1e-05)
    return (flat * scale * norm_gain).astype(jnp.bfloat16)

def reference(conv_input, step_raw, conv_weight, conv_bias, step_bias, decay_rate, norm_gain):
    total_rows, conv_dim = conv_input.shape
    head_count = decay_rate.shape[0]
    inner = norm_gain.shape[0]
    state_dim = (conv_dim - inner) // 2
    head_size = inner // head_count
    margin = conv_weight.shape[0] - 1
    padded = jnp.concatenate([jnp.zeros((margin, conv_dim), jnp.bfloat16), conv_input], axis=0)
    mixed = conv_mix(padded, conv_weight, conv_bias, total_rows)
    step_sizes = jax.nn.softplus(step_raw.astype(jnp.float32) + step_bias)
    log_decay = -decay_rate * step_sizes
    blocks = total_rows // GROUP
    values = mixed[:, :inner].reshape(blocks, GROUP, head_count, head_size)
    inputs_b = mixed[:, inner:inner + state_dim].reshape(blocks, GROUP, state_dim)
    inputs_c = mixed[:, inner + state_dim:].reshape(blocks, GROUP, state_dim)

    def advance(carried, pieces):
        block_values, block_b, block_c, block_steps, block_logs = pieces
        cumulative, within, update = block_parts(block_values, block_b, block_c, block_steps, block_logs)
        across = jnp.einsum('hpn,tn->thp', carried, block_c.astype(jnp.float32), precision=lax.Precision.HIGHEST)
        across = across * jnp.exp(cumulative)[:, :, None]
        result = finish(within + across, norm_gain)
        carried = jnp.exp(cumulative[-1])[:, None, None] * carried + update
        return (carried, result)
    start_state = jnp.zeros((head_count, head_size, state_dim), jnp.float32)
    final_state, outputs = lax.scan(advance, start_state, (values, inputs_b, inputs_c, step_sizes.reshape(blocks, GROUP, head_count), log_decay.reshape(blocks, GROUP, head_count)))
    return outputs.reshape(total_rows, inner)
```

```python
import functools

import jax
import jax.numpy as jnp
from jax import lax
from jax.experimental import pallas as pl
from jax.experimental.pallas import tpu as pltpu
from jax.sharding import PartitionSpec as P

GROUP = 256
WIDE = 256
HALO = 8
F32, BF16 = jnp.float32, jnp.bfloat16


def dot(left, right):
    return jnp.dot(left, right, preferred_element_type=F32)


def split(value):
    high = value.astype(BF16).astype(F32)
    return high, value - high


def lower_triangle():
    rows = lax.broadcasted_iota(jnp.int32, (GROUP, GROUP), 0)
    columns = lax.broadcasted_iota(jnp.int32, (GROUP, GROUP), 1)
    return rows >= columns


def front_kernel(
    inner, heads,
    before_ref, input_ref, raw_ref, weight_ref, bias_ref, step_bias_ref, rate_ref, spread_ref,
    xb_ref, bc_ref, a_ref, g_ref, state_ref, decay_ref,
    buf, pack,
):
    block = pl.program_id(0)

    @pl.when(block == 0)
    def _():
        buf[0:HALO] = before_ref[...].astype(F32)
        pack[...] = jnp.zeros_like(pack)
        state_ref[...] = jnp.zeros_like(state_ref)
        decay_ref[...] = jnp.ones_like(decay_ref)

    @pl.when(block > 0)
    def _():
        buf[0:HALO] = buf[GROUP : GROUP + HALO]

    half = pack.shape[1] // 2

    def packed(value):
        high, low = split(value)
        rows = value.shape[0]
        pack[0:rows, 0:heads] = high
        pack[0:rows, half : half + heads] = low
        return pack[0:rows, :].astype(BF16)

    shifted = raw_ref[...].astype(F32) + step_bias_ref[...]
    step = jnp.maximum(shifted, 0.0) + jnp.log(1.0 + jnp.exp(-jnp.abs(shifted)))
    logs = -rate_ref[...] * step
    ones = lower_triangle().astype(BF16)
    high, rest = split(logs)
    middle, low = split(rest)
    cum = dot(ones, high.astype(BF16)) + (
        dot(ones, middle.astype(BF16)) + dot(ones, low.astype(BF16))
    )
    mid = 0.5 * cum[GROUP - 1 : GROUP]
    a_ref[...] = packed(jnp.exp(cum - mid))
    g_pack = packed(jnp.exp(jnp.broadcast_to(mid, (8, heads))))
    b_pack = packed(jnp.exp(mid - cum) * step)

    def mix(columns):
        buf[HALO : HALO + GROUP, columns] = input_ref[:, columns].astype(F32)
        total = bias_ref[:, columns] + buf[HALO - 3 : HALO - 3 + GROUP, columns] * weight_ref[0:1, columns]
        for k in range(1, 4):
            total = total + buf[HALO - 3 + k : HALO - 3 + k + GROUP, columns] * weight_ref[k : k + 1, columns]
        part = 0.5 * total
        return (part + part * jnp.tanh(part)).astype(BF16)

    bc = mix(slice(inner, inner + WIDE))
    bc_ref[...] = bc
    b_turned = bc[:, : WIDE // 2].astype(F32).T.astype(BF16)

    for j in range(inner // WIDE):
        columns = slice(j * WIDE, (j + 1) * WIDE)
        spread = spread_ref[:, columns]
        xb = (mix(columns).astype(F32) * dot(b_pack, spread)).astype(BF16)
        xb_ref[:, columns] = xb
        g8 = dot(g_pack, spread)
        g_ref[:, columns] = g8
        g = g8[0:1]
        state_ref[:, columns] = g * (g * state_ref[:, columns] + dot(b_turned, xb))
        decay_ref[:, columns] = decay_ref[:, columns] * (g8 * g8)


def back_kernel(
    inner,
    xb_ref, bc_ref, a_ref, g_ref, spread_ref, incoming_ref, gain_ref,
    out_ref,
    state, rows,
):
    @pl.when(pl.program_id(0) == 0)
    def _():
        state[...] = incoming_ref[...].astype(F32)

    bc = bc_ref[...]
    width = WIDE // 2
    b, c = bc[:, :width], bc[:, width:]
    b_turned = b.astype(F32).T.astype(BF16)
    scores = dot(c, b_turned)
    scores = jnp.where(lower_triangle(), scores, 0.0).astype(BF16)
    c_twice = jnp.concatenate([c, c], axis=1)
    a_pack = a_ref[...]
    squares = jnp.zeros((GROUP, WIDE), F32)
    for j in range(inner // WIDE):
        columns = slice(j * WIDE, (j + 1) * WIDE)
        xb = xb_ref[:, columns]
        g = g_ref[0:1, columns]
        held = g * state[:, columns]
        high = held.astype(BF16)
        low = (held - high.astype(F32)).astype(BF16)
        total = dot(scores, xb) + dot(c_twice, jnp.concatenate([high, low], axis=0))
        y = total * dot(a_pack, spread_ref[:, columns])
        rows[:, columns] = y
        squares = squares + y * y
        state[:, columns] = g * (held + dot(b_turned, xb))
    mean = jnp.sum(squares, axis=1, keepdims=True) * (1.0 / inner)
    scale = lax.rsqrt(mean + 1e-05)
    for j in range(inner // WIDE):
        columns = slice(j * WIDE, (j + 1) * WIDE)
        out_ref[:, columns] = (rows[:, columns] * scale * gain_ref[:, columns]).astype(BF16)


def shift_pairs(count, stride):
    return [(d, d ^ stride) for d in range(count)]


def entering(state, decay, axis):
    count, place = lax.axis_size(axis), lax.axis_index(axis)
    levels = count.bit_length() - 1
    kept = []
    for level in range(levels - 1):
        stride = 1 << level
        pairs = shift_pairs(count, stride)
        right = ((place >> level) & 1) == 1
        rows = state.shape[0] // 2
        top, bottom = state[:rows], state[rows:]
        mine = jnp.where(right, bottom, top)
        sent = jnp.where(right, top, bottom).astype(BF16)
        got = lax.ppermute(sent, axis, pairs).astype(F32)
        other = lax.ppermute(decay, axis, pairs)
        first, second = jnp.where(right, got, mine), jnp.where(right, mine, got)
        first_decay, second_decay = jnp.where(right, other, decay), jnp.where(right, decay, other)
        kept.append((right, pairs, first, first_decay))
        state, decay = second_decay * first + second, first_decay * second_decay
    stride = count // 2
    prefix = lax.ppermute(state.astype(BF16), axis, [(d, d + stride) for d in range(stride)]).astype(F32)
    for right, pairs, first, first_decay in reversed(kept):
        later = first_decay * prefix + first
        keep = jnp.where(right, later, prefix)
        sent = jnp.where(right, prefix, later).astype(BF16)
        got = lax.ppermute(sent, axis, pairs).astype(F32)
        prefix = jnp.concatenate([jnp.where(right, got, keep), jnp.where(right, keep, got)], axis=0)
    return prefix


def per_device(conv_input, step_raw, conv_weight, conv_bias, step_bias, decay_rate, norm_gain):
    tokens, conv_dim = conv_input.shape
    heads, inner = decay_rate.shape[0], norm_gain.shape[0]
    width = (conv_dim - inner) // 2
    blocks = tokens // GROUP
    count = lax.axis_size("seq")
    before = lax.ppermute(conv_input[tokens - HALO :], "seq", [(d, d + 1) for d in range(count - 1)])
    owner = lax.broadcasted_iota(jnp.int32, (64, inner), 1) // (inner // heads)
    one = (owner == lax.broadcasted_iota(jnp.int32, (64, inner), 0)).astype(BF16)
    spread = jnp.concatenate([one, one], axis=0)

    def whole(*shape):
        return pl.BlockSpec(shape, lambda i: (0, 0))

    def stepped(*shape):
        return pl.BlockSpec(shape, lambda i: (i, 0))

    shape = jax.ShapeDtypeStruct
    xb, bc, a, g, state, decay = pl.pallas_call(
        functools.partial(front_kernel, inner, heads),
        grid=(blocks,),
        in_specs=[
            whole(HALO, conv_dim), stepped(GROUP, conv_dim), stepped(GROUP, heads),
            whole(4, conv_dim), whole(1, conv_dim), whole(1, heads), whole(1, heads),
            whole(128, inner),
        ],
        out_specs=[
            stepped(GROUP, inner), stepped(GROUP, WIDE), stepped(GROUP, 128), stepped(8, inner),
            whole(width, inner), whole(8, inner),
        ],
        out_shape=[
            shape((tokens, inner), BF16), shape((tokens, WIDE), BF16), shape((tokens, 128), BF16),
            shape((8 * blocks, inner), F32), shape((width, inner), F32), shape((8, inner), F32),
        ],
        scratch_shapes=[pltpu.VMEM((HALO + GROUP, conv_dim), F32), pltpu.VMEM((GROUP, 128), F32)],
        name="front",
    )(
        before, conv_input, step_raw, conv_weight, conv_bias[None], step_bias[None],
        decay_rate[None], spread,
    )
    incoming = entering(state, decay[0:1], "seq")
    return pl.pallas_call(
        functools.partial(back_kernel, inner),
        grid=(blocks,),
        in_specs=[
            stepped(GROUP, inner), stepped(GROUP, WIDE), stepped(GROUP, 128), stepped(8, inner),
            whole(128, inner), whole(width, inner), whole(1, inner),
        ],
        out_specs=stepped(GROUP, inner),
        out_shape=shape((tokens, inner), BF16),
        scratch_shapes=[pltpu.VMEM((width, inner), F32), pltpu.VMEM((GROUP, inner), F32)],
        name="back",
    )(xb, bc, a, g, spread, incoming, norm_gain[None])


def solution(mesh):
    placed = (P(("parts", "seq"), None), P(("parts", "seq"), None), P(), P(), P(), P(), P())
    return jax.shard_map(
        per_device, mesh=mesh, in_specs=placed, out_specs=P(("parts", "seq"), None), check_vma=False
    )
```

```python
import functools

import jax
import jax.numpy as jnp
from jax import lax
from jax.experimental import pallas as pl
from jax.experimental.pallas import tpu as pltpu
from jax.sharding import PartitionSpec as P

GROUP = 256
WIDE = 256
LANES = 128
PARTS = 2
HALO = 8
F32, BF16 = jnp.float32, jnp.bfloat16


def dot(left, right):
    return jnp.dot(left, right, preferred_element_type=F32)


def split(value):
    high = value.astype(BF16).astype(F32)
    return high, value - high


def lower_triangle():
    rows = lax.broadcasted_iota(jnp.int32, (GROUP, GROUP), 0)
    columns = lax.broadcasted_iota(jnp.int32, (GROUP, GROUP), 1)
    return rows >= columns


def fill_spread(spread, heads):
    width = spread.shape[1] // heads
    rows = lax.broadcasted_iota(jnp.int32, spread.shape, 0)
    columns = lax.broadcasted_iota(jnp.int32, spread.shape, 1)
    rows = jnp.where(rows >= LANES // 2, rows - LANES // 2, rows)
    start = rows * width
    spread[...] = jnp.where((columns >= start) & (columns < start + width), 1.0, 0.0).astype(BF16)


def front_kernel(
    inner, heads, blocks, count,
    before_ref, input_ref, whole_ref, raw_ref, weight_ref, bias_ref, step_bias_ref, rate_ref,
    xb_ref, bc_ref, a_ref, g_ref, state_ref,
    buf, halo, spread, pack, square, b_packs, g_packs, log_send, log_recv, log_first, log_second, wide_decay,
    keep, down_send, down_recv, top_send, top_recv, up_send, up_recv,
    halo_sems, log_sems, down_sems, top_sems, up_sems,
):
    at = pl.program_id(0)
    place = lax.axis_index("seq")
    levels = count.bit_length() - 1
    halvings = levels - 1
    half = LANES // 2
    tokens = blocks * GROUP
    rights = [lax.rem(place // (1 << level), 2) for level in range(levels)]
    partners = [place + (1 << level) * (1 - 2 * rights[level]) for level in range(levels)]
    behind, ahead = lax.rem(place + count - 1, count), lax.rem(place + 1, count)

    def send(source, target, sems, device):
        return pltpu.make_async_remote_copy(
            src_ref=source, dst_ref=target, send_sem=sems.at[0], recv_sem=sems.at[1],
            device_id={"seq": device}, device_id_type=pl.DeviceIdType.MESH,
        )

    halo_copy = send(whole_ref.at[pl.ds(tokens - 16, 16)], halo, halo_sems, ahead)

    def log_copy(level):
        return send(log_send.at[level], log_recv.at[level], log_sems.at[level], partners[level])

    def log_finish(level):
        log_copy(level).wait()
        own, other = log_send[level], log_recv[level]
        log_first[level] = jnp.where(rights[level] == 1, other, own)
        log_second[level] = jnp.where(rights[level] == 1, own, other)
        if level + 1 < halvings:
            log_send[level + 1] = own + other
            log_copy(level + 1).start()

    def turned(high, low):
        square[0:heads] = jnp.broadcast_to(high, (heads, LANES))
        square[half : half + heads] = jnp.broadcast_to(low, (heads, LANES))
        return square[...].T[0:8]

    def column(ref):
        square[0:1, 0:heads] = ref[...].reshape(1, heads)
        return jnp.broadcast_to(square[0:1], (LANES, LANES)).T[0:heads, 0:1]

    @pl.when(at == 0)
    def _():
        barrier = pltpu.get_barrier_semaphore()
        for device in partners + [behind, ahead]:
            pl.semaphore_signal(barrier, inc=1, device_id={"seq": device}, device_id_type=pl.DeviceIdType.MESH)
        square[...] = jnp.zeros_like(square)
        pack[...] = jnp.zeros_like(pack)
        step_bias, rate = column(step_bias_ref), column(rate_ref)
        square[...] = jnp.zeros_like(square)
        shifted = raw_ref[...].astype(F32) + step_bias
        step = jnp.maximum(shifted, 0.0) + jnp.log(1.0 + jnp.exp(-jnp.abs(shifted)))
        logs = -rate * step
        total = jnp.sum(logs, axis=1, keepdims=True)
        log_send[0] = turned(total, jnp.zeros_like(total))
        pl.semaphore_wait(barrier, levels + 2)
        if halvings > 0:
            log_copy(0).start()
        halo_copy.start()
        fill_spread(spread, heads)
        state_ref[...] = jnp.zeros_like(state_ref)
        ones = lower_triangle().astype(F32).T.astype(BF16)
        high, rest = split(logs)
        middle, low = split(rest)
        for block in range(blocks):
            span = slice(block * GROUP, (block + 1) * GROUP)
            cum = dot(high[:, span].astype(BF16), ones) + (
                dot(middle[:, span].astype(BF16), ones) + dot(low[:, span].astype(BF16), ones)
            )
            mid = 0.5 * cum[:, GROUP - 1 : GROUP]
            first, second = split(jnp.exp(cum - mid))
            pack[0:heads, :] = first
            pack[half : half + heads, :] = second
            a_ref[span] = pack[...].T.astype(BF16)
            first, second = split(jnp.exp(mid - cum) * step[:, span])
            pack[0:heads, :] = first
            pack[half : half + heads, :] = second
            b_packs[span] = pack[...].T.astype(BF16)
            first, second = split(jnp.exp(mid))
            g_packs[8 * block : 8 * block + 8] = turned(first, second)

    @pl.when(at < blocks - 1)
    def _():
        buf[0:HALO] = before_ref[HALO : 2 * HALO].astype(F32)

    for level in range(min(halvings, blocks - 2)):
        @pl.when(at == level + 1)
        def _():
            log_finish(level)

    last = at == blocks - 1

    @pl.when(last)
    def _():
        for level in range(min(halvings, blocks - 2), halvings):
            log_finish(level)
        halo_copy.wait()
        buf[0:HALO] = jnp.where(place == 0, 0.0, halo[HALO : 2 * HALO].astype(F32))

    block = lax.rem(at + 1, blocks)
    b_pack = b_packs[pl.ds(pl.multiple_of(block * GROUP, GROUP), GROUP)]
    g_pack = g_packs[pl.ds(pl.multiple_of(block * 8, 8), 8)].astype(BF16)

    def mix(columns):
        buf[HALO : HALO + GROUP, columns] = input_ref[:, columns].astype(F32)
        total = bias_ref[columns].reshape(1, WIDE) + buf[HALO - 3 : HALO - 3 + GROUP, columns] * weight_ref[0:1, columns]
        for k in range(1, 4):
            total = total + buf[HALO - 3 + k : HALO - 3 + k + GROUP, columns] * weight_ref[k : k + 1, columns]
        part = 0.5 * total
        return (part + part * jnp.tanh(part)).astype(BF16)

    bc = mix(slice(inner, inner + WIDE))
    bc_ref[...] = bc
    b_turned = bc[:, : WIDE // 2].astype(F32).T.astype(BF16)

    def chunk(j):
        columns = slice(j * WIDE, (j + 1) * WIDE)
        wide = spread[:, columns]
        xb = (mix(columns).astype(F32) * dot(b_pack, wide)).astype(BF16)
        xb_ref[:, columns] = xb
        g8 = dot(g_pack, wide)
        g_ref[:, columns] = g8
        return columns, g8[0:1], dot(b_turned, xb)

    @pl.when(at < blocks - 1)
    def _():
        for j in range(inner // WIDE):
            columns, g, update = chunk(j)
            state_ref[:, columns] = g * (g * state_ref[:, columns] + update)
            wide_decay[0:8, columns] = jnp.where(at == 0, 1.0, wide_decay[0:8, columns]) * (g * g)

    group = inner // PARTS

    def part_of(part):
        return slice(part * group, (part + 1) * group)

    def rows_of(level):
        return LANES >> (level + 1)

    def decay_row(level, which, columns):
        row = 8 + 16 * level + 8 * which
        return wide_decay[row : row + 1, columns]

    def down_copy(level, part):
        return send(down_send[level].at[part], down_recv[level].at[part], down_sems.at[level, part], partners[level])

    def up_copy(level, part):
        return send(up_send[level].at[part], up_recv[level].at[part], up_sems.at[level, part], partners[level])

    def top_copy(part):
        return send(top_send.at[part], top_recv.at[part], top_sems.at[part], partners[levels - 1])

    def down_start(level, part):
        if level == halvings:
            top_send[part] = state_ref[0 : LANES >> level, part_of(part)].astype(BF16)
            top_copy(part).start()
            return
        rows, columns, right = rows_of(level), part_of(part), rights[level] == 1
        top, bottom = state_ref[0:rows, columns], state_ref[rows : 2 * rows, columns]
        down_send[level][part] = jnp.where(right, top, bottom).astype(BF16)
        down_copy(level, part).start()
        keep[level][:, columns] = jnp.where(right, bottom, top)

    def down_finish(level, part):
        rows, columns, right = rows_of(level), part_of(part), rights[level] == 1
        down_copy(level, part).wait()
        got, mine = down_recv[level][part].astype(F32), keep[level][:, columns]
        first, second = jnp.where(right, got, mine), jnp.where(right, mine, got)
        state_ref[0:rows, columns] = decay_row(level, 1, columns) * first + second
        keep[level][:, columns] = first

    def up_start(level, part):
        rows, columns, right = rows_of(level), part_of(part), rights[level] == 1
        prefix = state_ref[0:rows, columns]
        later = decay_row(level, 0, columns) * prefix + keep[level][:, columns]
        up_send[level][part] = jnp.where(right, prefix, later).astype(BF16)
        up_copy(level, part).start()
        keep[level][:, columns] = jnp.where(right, later, prefix)

    def up_finish(level, part):
        rows, columns, right = rows_of(level), part_of(part), rights[level] == 1
        up_copy(level, part).wait()
        got, mine = up_recv[level][part].astype(F32), keep[level][:, columns]
        state_ref[0:rows, columns] = jnp.where(right, got, mine)
        state_ref[rows : 2 * rows, columns] = jnp.where(right, mine, got)

    @pl.when(last)
    def _():
        decays = []
        for level in range(halvings):
            for log in (log_first[level], log_second[level]):
                first, second = split(jnp.exp(log))
                lane = lax.broadcasted_iota(jnp.int32, (8, LANES), 1)
                decays.append(jnp.where(lane < half, first, pltpu.roll(second, half, 1)))
        decay_pack = jnp.concatenate(decays, axis=0).astype(BF16)
        for j in range(inner // WIDE):
            columns, g, update = chunk(j)
            state_ref[:, columns] = state_ref[:, columns] + wide_decay[0:1, columns] * (g * update)
            wide_decay[8 : 8 + 16 * halvings, columns] = dot(decay_pack, spread[:, columns])
            for part in range(PARTS):
                if (part + 1) * group == (j + 1) * WIDE:
                    down_start(0, part)
        for level in range(halvings):
            for part in range(PARTS):
                down_finish(level, part)
                down_start(level + 1, part)
        for part in range(PARTS):
            top_copy(part).wait()
            state_ref[0 : LANES >> halvings, part_of(part)] = jnp.where(
                rights[levels - 1] == 1, top_recv[part].astype(F32), 0.0
            )
            up_start(halvings - 1, part)
        for level in reversed(range(halvings)):
            for part in range(PARTS):
                up_finish(level, part)
                if level > 0:
                    up_start(level - 1, part)


def back_kernel(
    inner, heads,
    xb_ref, bc_ref, a_ref, g_ref, incoming_ref, gain_ref,
    out_ref,
    state, rows, spread,
):
    @pl.when(pl.program_id(0) == 0)
    def _():
        state[...] = incoming_ref[...]
        fill_spread(spread, heads)

    bc = bc_ref[...]
    width = WIDE // 2
    b, c = bc[:, :width], bc[:, width:]
    b_turned = b.astype(F32).T.astype(BF16)
    scores = dot(c, b_turned)
    scores = jnp.where(lower_triangle(), scores, 0.0).astype(BF16)
    c_twice = jnp.concatenate([c, c], axis=1)
    a_pack = a_ref[...]
    squares = jnp.zeros((GROUP, WIDE), F32)
    for j in range(inner // WIDE):
        columns = slice(j * WIDE, (j + 1) * WIDE)
        xb = xb_ref[:, columns]
        g = g_ref[0:1, columns]
        held = g * state[:, columns]
        high = held.astype(BF16)
        low = (held - high.astype(F32)).astype(BF16)
        total = dot(scores, xb) + dot(c_twice, jnp.concatenate([high, low], axis=0))
        y = total * dot(a_pack, spread[:, columns])
        rows[:, columns] = y
        squares = squares + y * y
        state[:, columns] = g * (held + dot(b_turned, xb))
    mean = jnp.sum(squares, axis=1, keepdims=True) * (1.0 / inner)
    scale = lax.rsqrt(mean + 1e-05)
    for j in range(inner // WIDE):
        columns = slice(j * WIDE, (j + 1) * WIDE)
        out_ref[:, columns] = (rows[:, columns] * scale * gain_ref[columns].reshape(1, WIDE)).astype(BF16)


def per_device(conv_input, step_raw, conv_weight, conv_bias, step_bias, decay_rate, norm_gain):
    tokens, conv_dim = conv_input.shape
    heads, inner = decay_rate.shape[0], norm_gain.shape[0]
    blocks = tokens // GROUP
    count = lax.axis_size("seq")
    levels = count.bit_length() - 1
    halvings = levels - 1
    group = inner // PARTS
    sizes = [LANES >> (level + 1) for level in range(halvings)]

    def whole(*shape):
        return pl.BlockSpec(shape, lambda i: (0,) * len(shape))

    def stepped(*shape):
        return pl.BlockSpec(shape, lambda i: (i, 0))

    def turned(*shape):
        return pl.BlockSpec(shape, lambda i: (lax.rem(i + 1, blocks), 0))

    def vmem(*shape, dtype=F32):
        return pltpu.VMEM(shape, dtype)

    slots = [vmem(PARTS, rows, group, dtype=BF16) for rows in sizes]
    shape = jax.ShapeDtypeStruct
    xb, bc, a, g, state = pl.pallas_call(
        functools.partial(front_kernel, inner, heads, blocks, count),
        grid=(blocks,),
        in_specs=[
            pl.BlockSpec((16, conv_dim), lambda i: (jnp.maximum(lax.rem(i + 1, blocks) * (GROUP // 16) - 1, 0), 0)),
            turned(GROUP, conv_dim), pl.BlockSpec(memory_space=pl.ANY),
            whole(heads, tokens), whole(4, conv_dim), whole(conv_dim), whole(heads), whole(heads),
        ],
        out_specs=[
            turned(GROUP, inner), turned(GROUP, WIDE), whole(tokens, LANES), turned(8, inner),
            whole(LANES, inner),
        ],
        out_shape=[
            shape((tokens, inner), BF16), shape((tokens, WIDE), BF16), shape((tokens, LANES), BF16),
            shape((8 * blocks, inner), F32), shape((LANES, inner), F32),
        ],
        scratch_shapes=[
            vmem(HALO + GROUP, conv_dim), vmem(16, conv_dim, dtype=BF16), vmem(LANES, inner, dtype=BF16),
            vmem(LANES, GROUP), vmem(LANES, LANES), vmem(tokens, LANES, dtype=BF16), vmem(8 * blocks, LANES),
            vmem(halvings, 8, LANES), vmem(halvings, 8, LANES), vmem(halvings, 8, LANES), vmem(halvings, 8, LANES),
            vmem(8 + 16 * halvings, inner),
            [vmem(rows, inner) for rows in sizes], slots, slots,
            vmem(PARTS, LANES >> halvings, group, dtype=BF16), vmem(PARTS, LANES >> halvings, group, dtype=BF16),
            slots, slots,
            pltpu.SemaphoreType.DMA((2,)), pltpu.SemaphoreType.DMA((halvings, 2)),
            pltpu.SemaphoreType.DMA((halvings, PARTS, 2)), pltpu.SemaphoreType.DMA((PARTS, 2)),
            pltpu.SemaphoreType.DMA((halvings, PARTS, 2)),
        ],
        compiler_params=pltpu.CompilerParams(collective_id=0, has_side_effects=True, vmem_limit_bytes=60 * 1024 * 1024),
        name="front",
    )(conv_input, conv_input, conv_input, step_raw.T, conv_weight, conv_bias, step_bias, decay_rate)
    return pl.pallas_call(
        functools.partial(back_kernel, inner, heads),
        grid=(blocks,),
        in_specs=[
            stepped(GROUP, inner), stepped(GROUP, WIDE), stepped(GROUP, LANES), stepped(8, inner),
            whole(LANES, inner), whole(inner),
        ],
        out_specs=stepped(GROUP, inner),
        out_shape=shape((tokens, inner), BF16),
        scratch_shapes=[vmem(LANES, inner), vmem(GROUP, inner), vmem(LANES, inner, dtype=BF16)],
        name="back",
    )(xb, bc, a, g, state, norm_gain)


def solution(mesh):
    placed = (P(("parts", "seq"), None), P(("parts", "seq"), None), P(), P(), P(), P(), P())
    return jax.shard_map(
        per_device, mesh=mesh, in_specs=placed, out_specs=P(("parts", "seq"), None), check_vma=False
    )
```

```python
import functools

import jax
import jax.numpy as jnp
from jax import lax
from jax.experimental import pallas as pl
from jax.experimental.pallas import tpu as pltpu
from jax.sharding import PartitionSpec as P

GROUP = 256
WIDE = 256
LANES = 128
PARTS = 5
HALO = 8
F32, BF16 = jnp.float32, jnp.bfloat16


def dot(left, right):
    return jnp.dot(left, right, preferred_element_type=F32)


def split(value):
    high = value.astype(BF16).astype(F32)
    return high, value - high


def lower_triangle():
    rows = lax.broadcasted_iota(jnp.int32, (GROUP, GROUP), 0)
    columns = lax.broadcasted_iota(jnp.int32, (GROUP, GROUP), 1)
    return rows >= columns


def fill_spread(spread, heads):
    width = spread.shape[1] // heads
    rows = lax.broadcasted_iota(jnp.int32, spread.shape, 0)
    columns = lax.broadcasted_iota(jnp.int32, spread.shape, 1)
    rows = jnp.where(rows >= LANES // 2, rows - LANES // 2, rows)
    start = rows * width
    spread[...] = jnp.where((columns >= start) & (columns < start + width), 1.0, 0.0).astype(BF16)


def front_kernel(
    inner, heads, blocks, count,
    input_ref, bc_in_ref, whole_ref, raw_ref, weight_ref, bias_ref, step_bias_ref, rate_ref,
    xb_ref, bc_ref, a_ref, g_ref, state_ref,
    bias, b_turned, halo, spread, pack, square, b_packs, g_packs, log_send, log_recv, log_first, log_second, wide_decay,
    keep, down_send, down_recv, top_send, top_recv, up_send, up_recv,
    halo_sems, log_sems, down_sems, top_sems, up_sems,
):
    at = pl.program_id(0)
    place = lax.axis_index("seq")
    levels = count.bit_length() - 1
    halvings = levels - 1
    half = LANES // 2
    tokens = blocks * GROUP
    rights = [lax.rem(place // (1 << level), 2) for level in range(levels)]
    partners = [place + (1 << level) * (1 - 2 * rights[level]) for level in range(levels)]
    behind, ahead = lax.rem(place + count - 1, count), lax.rem(place + 1, count)

    def send(source, target, sems, device):
        return pltpu.make_async_remote_copy(
            src_ref=source, dst_ref=target, send_sem=sems.at[0], recv_sem=sems.at[1],
            device_id={"seq": device}, device_id_type=pl.DeviceIdType.MESH,
        )

    halo_copy = send(whole_ref.at[pl.ds(tokens - 16, 16)], halo, halo_sems, ahead)

    def log_copy(level):
        return send(log_send.at[level], log_recv.at[level], log_sems.at[level], partners[level])

    def log_finish(level):
        log_copy(level).wait()
        own, other = log_send[level], log_recv[level]
        log_first[level] = jnp.where(rights[level] == 1, other, own)
        log_second[level] = jnp.where(rights[level] == 1, own, other)
        if level + 1 < halvings:
            log_send[level + 1] = own + other
            log_copy(level + 1).start()

    def turned(high, low):
        square[0:heads] = jnp.broadcast_to(high, (heads, LANES))
        square[half : half + heads] = jnp.broadcast_to(low, (heads, LANES))
        return square[...].T[0:8]

    def column(ref):
        square[0:1, 0:heads] = ref[...].reshape(1, heads)
        return jnp.broadcast_to(square[0:1], (LANES, LANES)).T[0:heads, 0:1]

    @pl.when(at == 0)
    def _():
        barrier = pltpu.get_barrier_semaphore()
        for device in partners + [behind, ahead]:
            pl.semaphore_signal(barrier, inc=1, device_id={"seq": device}, device_id_type=pl.DeviceIdType.MESH)
        square[...] = jnp.zeros_like(square)
        pack[...] = jnp.zeros_like(pack)
        step_bias, rate = column(step_bias_ref), column(rate_ref)
        square[...] = jnp.zeros_like(square)
        shifted = raw_ref[...].astype(F32) + step_bias
        step = jnp.maximum(shifted, 0.0) + jnp.log(1.0 + jnp.exp(-jnp.abs(shifted)))
        logs = -rate * step
        total = jnp.sum(logs, axis=1, keepdims=True)
        log_send[0] = turned(total, jnp.zeros_like(total))
        pl.semaphore_wait(barrier, levels + 2)
        if halvings > 0:
            log_copy(0).start()
        halo_copy.start()
        fill_spread(spread, heads)
        bias[...] = 0.5 * bias_ref[...].reshape(1, bias.shape[1])
        ones = lower_triangle().astype(F32).T.astype(BF16)
        high, rest = split(logs)
        middle, low = split(rest)
        for block in range(blocks):
            span = slice(block * GROUP, (block + 1) * GROUP)
            cum = dot(high[:, span].astype(BF16), ones) + (
                dot(middle[:, span].astype(BF16), ones) + dot(low[:, span].astype(BF16), ones)
            )
            mid = 0.5 * cum[:, GROUP - 1 : GROUP]
            first, second = split(jnp.exp(cum - mid))
            pack[0:heads, :] = first
            pack[half : half + heads, :] = second
            a_ref[span] = pack[...].T.astype(BF16)
            first, second = split(jnp.exp(mid - cum) * step[:, span])
            pack[0:heads, :] = first
            pack[half : half + heads, :] = second
            b_packs[span] = pack[...].T.astype(BF16)
            first, second = split(jnp.exp(mid))
            g_packs[8 * block : 8 * block + 8] = turned(first, second)

    def halo_rows(source, block, inside, lanes):
        if block == 0:
            return jnp.where(place == 0, 0.0, halo[HALO : 2 * HALO, lanes].astype(F32))
        return source[block * GROUP - 16 : block * GROUP, inside].astype(F32)[HALO:]

    def mix(source, block, inside, outside):
        pieces = []
        for start in range(0, WIDE, LANES):
            here = slice(inside + start, inside + start + LANES)
            lanes = pl.ds(pl.multiple_of(outside + start, LANES), LANES)
            span = slice(block * GROUP, (block + 1) * GROUP)
            rows = jnp.concatenate(
                [halo_rows(source, block, here, lanes), source[span, here].astype(F32)], axis=0
            )
            weights = 0.5 * weight_ref[:, lanes]
            total = rows * weights[0:1]
            for k in range(1, 4):
                total = pltpu.roll(total, 1, 0) + rows * weights[k : k + 1]
            part = total[HALO:] + bias[:, lanes]
            pieces.append((part + part * jnp.tanh(part)).astype(BF16))
        return jnp.concatenate(pieces, axis=1)

    order = list(range(1, blocks)) + [0]

    @pl.when(at == 0)
    def _():
        for block in order:
            if block == 0:
                halo_copy.wait()
            bc = mix(bc_in_ref, block, 0, inner)
            bc_ref[block * GROUP : (block + 1) * GROUP] = bc
            b_turned[block] = bc[:, : WIDE // 2].astype(F32).T.astype(BF16)

    def widen(level):
        decays = []
        lane = lax.broadcasted_iota(jnp.int32, (8, LANES), 1)
        for log in (log_first[level], log_second[level]):
            first, second = split(jnp.exp(log))
            decays.append(jnp.where(lane < half, first, pltpu.roll(second, half, 1)))
        decay_pack = jnp.concatenate(decays, axis=0).astype(BF16)
        for j in range(inner // WIDE):
            columns = slice(j * WIDE, (j + 1) * WIDE)
            wide_decay[16 * level : 16 * level + 16, columns] = dot(decay_pack, spread[:, columns])

    for step_at in range(1, PARTS):
        @pl.when(at == step_at)
        def _():
            stop = halvings if step_at == PARTS - 1 else min(step_at, halvings)
            for level in range(min(step_at - 1, halvings), stop):
                log_finish(level)
                widen(level)

    for j in range(inner // PARTS // WIDE):
        outside = pl.multiple_of(at * (inner // PARTS) + j * WIDE, WIDE)
        columns = pl.ds(outside, WIDE)
        here = slice(j * WIDE, (j + 1) * WIDE)
        wide = spread[:, columns]
        state, decay = None, None
        for block in order:
            span = slice(block * GROUP, (block + 1) * GROUP)
            xb = (mix(input_ref, block, j * WIDE, outside).astype(F32) * dot(b_packs[span], wide)).astype(BF16)
            xb_ref[span, here] = xb
            g8 = dot(g_packs[8 * block : 8 * block + 8].astype(BF16), wide)
            g_ref[8 * block : 8 * block + 8, here] = g8
            g = g8[0:1]
            update = g * dot(b_turned[block], xb)
            if block == 0:
                state = update if state is None else state + decay * update
            elif state is None:
                state, decay = update, g * g
            else:
                state, decay = (g * g) * state + update, decay * (g * g)
        state_ref[:, columns] = state

    group = inner // PARTS

    def part_of(part):
        return slice(part * group, (part + 1) * group)

    def rows_of(level):
        return LANES >> (level + 1)

    def decay_row(level, which, columns):
        row = 16 * level + 8 * which
        return wide_decay[row : row + 1, columns]

    def down_copy(level, part):
        return send(down_send[level].at[part], down_recv[level].at[part], down_sems.at[level, part], partners[level])

    def up_copy(level, part):
        return send(up_send[level].at[part], up_recv[level].at[part], up_sems.at[level, part], partners[level])

    def top_copy(part):
        return send(top_send.at[part], top_recv.at[part], top_sems.at[part], partners[levels - 1])

    def down_start(level, part):
        if level == halvings:
            top_send[part] = state_ref[0 : LANES >> level, part_of(part)].astype(BF16)
            top_copy(part).start()
            return
        rows, columns, right = rows_of(level), part_of(part), rights[level] == 1
        top, bottom = state_ref[0:rows, columns], state_ref[rows : 2 * rows, columns]
        down_send[level][part] = jnp.where(right, top, bottom).astype(BF16)
        down_copy(level, part).start()
        keep[level][:, columns] = jnp.where(right, bottom, top)

    def down_finish(level, part):
        rows, columns, right = rows_of(level), part_of(part), rights[level] == 1
        down_copy(level, part).wait()
        got, mine = down_recv[level][part].astype(F32), keep[level][:, columns]
        first, second = jnp.where(right, got, mine), jnp.where(right, mine, got)
        state_ref[0:rows, columns] = decay_row(level, 1, columns) * first + second
        keep[level][:, columns] = first

    def up_start(level, part):
        rows, columns, right = rows_of(level), part_of(part), rights[level] == 1
        prefix = state_ref[0:rows, columns]
        later = decay_row(level, 0, columns) * prefix + keep[level][:, columns]
        up_send[level][part] = jnp.where(right, prefix, later).astype(BF16)
        up_copy(level, part).start()
        keep[level][:, columns] = jnp.where(right, later, prefix)

    def up_finish(level, part):
        rows, columns, right = rows_of(level), part_of(part), rights[level] == 1
        up_copy(level, part).wait()
        got, mine = up_recv[level][part].astype(F32), keep[level][:, columns]
        state_ref[0:rows, columns] = jnp.where(right, got, mine)
        state_ref[rows : 2 * rows, columns] = jnp.where(right, mine, got)

    rounds = 2 * halvings + 1

    def advance(part, turn):
        if turn < halvings:
            down_finish(turn, part)
            down_start(turn + 1, part)
        elif turn == halvings:
            top_copy(part).wait()
            state_ref[0 : LANES >> halvings, part_of(part)] = jnp.where(
                rights[levels - 1] == 1, top_recv[part].astype(F32), 0.0
            )
            up_start(halvings - 1, part)
        else:
            level = 2 * halvings - turn
            up_finish(level, part)
            if level > 0:
                up_start(level - 1, part)

    for step_at in range(PARTS):
        @pl.when(at == step_at)
        def _():
            down_start(0, step_at)
            for part in range(step_at):
                if step_at - part - 1 < rounds:
                    advance(part, step_at - part - 1)
            if step_at == PARTS - 1:
                for wave in range(rounds):
                    for part in range(PARTS):
                        if PARTS - 1 - part + wave < rounds:
                            advance(part, PARTS - 1 - part + wave)


def back_kernel(
    inner, heads,
    xb_ref, bc_ref, a_ref, g_ref, incoming_ref, gain_ref,
    out_ref,
    state, rows, spread,
):
    @pl.when(pl.program_id(0) == 0)
    def _():
        state[...] = incoming_ref[...]
        fill_spread(spread, heads)

    bc = bc_ref[...]
    width = WIDE // 2
    b, c = bc[:, :width], bc[:, width:]
    b_turned = b.astype(F32).T.astype(BF16)
    scores = dot(c, b_turned)
    scores = jnp.where(lower_triangle(), scores, 0.0).astype(BF16)
    c_twice = jnp.concatenate([c, c], axis=1)
    a_pack = a_ref[...]
    squares = jnp.zeros((GROUP, WIDE), F32)
    for j in range(inner // WIDE):
        columns = slice(j * WIDE, (j + 1) * WIDE)
        xb = xb_ref[:, columns]
        g = g_ref[0:1, columns]
        held = g * state[:, columns]
        high = held.astype(BF16)
        low = (held - high.astype(F32)).astype(BF16)
        total = dot(scores, xb) + dot(c_twice, jnp.concatenate([high, low], axis=0))
        y = total * dot(a_pack, spread[:, columns])
        rows[:, columns] = y
        squares = squares + y * y
        state[:, columns] = g * (held + dot(b_turned, xb))
    mean = jnp.sum(squares, axis=1, keepdims=True) * (1.0 / inner)
    scale = lax.rsqrt(mean + 1e-05)
    for j in range(inner // WIDE):
        columns = slice(j * WIDE, (j + 1) * WIDE)
        out_ref[:, columns] = (rows[:, columns] * scale * gain_ref[columns].reshape(1, WIDE)).astype(BF16)


def per_device(conv_input, step_raw, conv_weight, conv_bias, step_bias, decay_rate, norm_gain):
    tokens, conv_dim = conv_input.shape
    heads, inner = decay_rate.shape[0], norm_gain.shape[0]
    blocks = tokens // GROUP
    count = lax.axis_size("seq")
    levels = count.bit_length() - 1
    halvings = levels - 1
    group = inner // PARTS
    sizes = [LANES >> (level + 1) for level in range(halvings)]

    def whole(*shape):
        return pl.BlockSpec(shape, lambda i: (0,) * len(shape))

    def stepped(*shape):
        return pl.BlockSpec(shape, lambda i: (i, 0))

    def sideways(*shape):
        return pl.BlockSpec(shape, lambda i: (0, i))

    def vmem(*shape, dtype=F32):
        return pltpu.VMEM(shape, dtype)

    slots = [vmem(PARTS, rows, group, dtype=BF16) for rows in sizes]
    shape = jax.ShapeDtypeStruct
    xb, bc, a, g, state = pl.pallas_call(
        functools.partial(front_kernel, inner, heads, blocks, count),
        grid=(PARTS,),
        in_specs=[
            sideways(tokens, group), pl.BlockSpec((tokens, WIDE), lambda i: (0, inner // WIDE)),
            pl.BlockSpec(memory_space=pl.ANY),
            whole(heads, tokens), whole(4, conv_dim), whole(conv_dim), whole(heads), whole(heads),
        ],
        out_specs=[
            sideways(tokens, group), whole(tokens, WIDE), whole(tokens, LANES), sideways(8 * blocks, group),
            whole(LANES, inner),
        ],
        out_shape=[
            shape((tokens, inner), BF16), shape((tokens, WIDE), BF16), shape((tokens, LANES), BF16),
            shape((8 * blocks, inner), F32), shape((LANES, inner), F32),
        ],
        scratch_shapes=[
            vmem(1, conv_dim), vmem(blocks, LANES, GROUP, dtype=BF16), vmem(16, conv_dim, dtype=BF16), vmem(LANES, inner, dtype=BF16),
            vmem(LANES, GROUP), vmem(LANES, LANES), vmem(tokens, LANES, dtype=BF16), vmem(8 * blocks, LANES),
            vmem(halvings, 8, LANES), vmem(halvings, 8, LANES), vmem(halvings, 8, LANES), vmem(halvings, 8, LANES),
            vmem(16 * halvings, inner),
            [vmem(rows, inner) for rows in sizes], slots, slots,
            vmem(PARTS, LANES >> halvings, group, dtype=BF16), vmem(PARTS, LANES >> halvings, group, dtype=BF16),
            slots, slots,
            pltpu.SemaphoreType.DMA((2,)), pltpu.SemaphoreType.DMA((halvings, 2)),
            pltpu.SemaphoreType.DMA((halvings, PARTS, 2)), pltpu.SemaphoreType.DMA((PARTS, 2)),
            pltpu.SemaphoreType.DMA((halvings, PARTS, 2)),
        ],
        compiler_params=pltpu.CompilerParams(collective_id=0, has_side_effects=True, vmem_limit_bytes=60 * 1024 * 1024),
        name="front",
    )(conv_input, conv_input, conv_input, step_raw.T, conv_weight, conv_bias, step_bias, decay_rate)
    return pl.pallas_call(
        functools.partial(back_kernel, inner, heads),
        grid=(blocks,),
        in_specs=[
            stepped(GROUP, inner), stepped(GROUP, WIDE), stepped(GROUP, LANES), stepped(8, inner),
            whole(LANES, inner), whole(inner),
        ],
        out_specs=stepped(GROUP, inner),
        out_shape=shape((tokens, inner), BF16),
        scratch_shapes=[vmem(LANES, inner), vmem(GROUP, inner), vmem(LANES, inner, dtype=BF16)],
        name="back",
    )(xb, bc, a, g, state, norm_gain)


def solution(mesh):
    placed = (P(("parts", "seq"), None), P(("parts", "seq"), None), P(), P(), P(), P(), P())
    return jax.shard_map(
        per_device, mesh=mesh, in_specs=placed, out_specs=P(("parts", "seq"), None), check_vma=False
    )
```

```python
import functools

import jax
import jax.numpy as jnp
from jax import lax
from jax.experimental import pallas as pl
from jax.experimental.pallas import tpu as pltpu
from jax.sharding import PartitionSpec as P

GROUP = 256
WIDE = 256
LANES = 128
PARTS = 2
HALO = 8
F32, BF16 = jnp.float32, jnp.bfloat16


def dot(left, right):
    return jnp.dot(left, right, preferred_element_type=F32)


def split(value):
    high = value.astype(BF16).astype(F32)
    return high, value - high


def lower_triangle():
    rows = lax.broadcasted_iota(jnp.int32, (GROUP, GROUP), 0)
    columns = lax.broadcasted_iota(jnp.int32, (GROUP, GROUP), 1)
    return rows >= columns


def fill_spread(spread, heads):
    width = spread.shape[1] // heads
    rows = lax.broadcasted_iota(jnp.int32, spread.shape, 0)
    columns = lax.broadcasted_iota(jnp.int32, spread.shape, 1)
    rows = jnp.where(rows >= LANES // 2, rows - LANES // 2, rows)
    start = rows * width
    spread[...] = jnp.where((columns >= start) & (columns < start + width), 1.0, 0.0).astype(BF16)


def front_kernel(
    inner, heads, blocks, count,
    before_ref, input_ref, whole_ref, raw_ref, weight_ref, bias_ref, step_bias_ref, rate_ref,
    xb_ref, bc_ref, a_ref, g_ref, state_ref,
    buf, halo, spread, pack, square, b_packs, g_packs, log_send, log_recv, log_first, log_second, wide_decay,
    keep, down_send, down_recv, top_send, top_recv, up_send, up_recv,
    halo_sems, log_sems, down_sems, top_sems, up_sems,
):
    at = pl.program_id(0)
    place = lax.axis_index("seq")
    levels = count.bit_length() - 1
    halvings = levels - 1
    half = LANES // 2
    tokens = blocks * GROUP
    rights = [lax.rem(place // (1 << level), 2) for level in range(levels)]
    partners = [place + (1 << level) * (1 - 2 * rights[level]) for level in range(levels)]
    behind, ahead = lax.rem(place + count - 1, count), lax.rem(place + 1, count)

    def send(source, target, sems, device):
        return pltpu.make_async_remote_copy(
            src_ref=source, dst_ref=target, send_sem=sems.at[0], recv_sem=sems.at[1],
            device_id={"seq": device}, device_id_type=pl.DeviceIdType.MESH,
        )

    halo_copy = send(whole_ref.at[pl.ds(tokens - 16, 16)], halo, halo_sems, ahead)

    def log_copy(level):
        return send(log_send.at[level], log_recv.at[level], log_sems.at[level], partners[level])

    def log_finish(level):
        log_copy(level).wait()
        own, other = log_send[level], log_recv[level]
        log_first[level] = jnp.where(rights[level] == 1, other, own)
        log_second[level] = jnp.where(rights[level] == 1, own, other)
        if level + 1 < halvings:
            log_send[level + 1] = own + other
            log_copy(level + 1).start()

    def turned(high, low):
        square[0:heads] = jnp.broadcast_to(high, (heads, LANES))
        square[half : half + heads] = jnp.broadcast_to(low, (heads, LANES))
        return square[...].T[0:8]

    def column(ref):
        square[0:1, 0:heads] = ref[...].reshape(1, heads)
        return jnp.broadcast_to(square[0:1], (LANES, LANES)).T[0:heads, 0:1]

    @pl.when(at == 0)
    def _():
        barrier = pltpu.get_barrier_semaphore()
        for device in partners + [behind, ahead]:
            pl.semaphore_signal(barrier, inc=1, device_id={"seq": device}, device_id_type=pl.DeviceIdType.MESH)
        square[...] = jnp.zeros_like(square)
        pack[...] = jnp.zeros_like(pack)
        step_bias, rate = column(step_bias_ref), column(rate_ref)
        square[...] = jnp.zeros_like(square)
        shifted = raw_ref[...].astype(F32) + step_bias
        step = jnp.maximum(shifted, 0.0) + jnp.log(1.0 + jnp.exp(-jnp.abs(shifted)))
        logs = -rate * step
        total = jnp.sum(logs, axis=1, keepdims=True)
        log_send[0] = turned(total, jnp.zeros_like(total))
        pl.semaphore_wait(barrier, levels + 2)
        if halvings > 0:
            log_copy(0).start()
        halo_copy.start()
        fill_spread(spread, heads)
        state_ref[...] = jnp.zeros_like(state_ref)
        ones = lower_triangle().astype(F32).T.astype(BF16)
        high, rest = split(logs)
        middle, low = split(rest)
        for block in range(blocks):
            span = slice(block * GROUP, (block + 1) * GROUP)
            cum = dot(high[:, span].astype(BF16), ones) + (
                dot(middle[:, span].astype(BF16), ones) + dot(low[:, span].astype(BF16), ones)
            )
            mid = 0.5 * cum[:, GROUP - 1 : GROUP]
            first, second = split(jnp.exp(cum - mid))
            pack[0:heads, :] = first
            pack[half : half + heads, :] = second
            a_ref[span] = pack[...].T.astype(BF16)
            first, second = split(jnp.exp(mid - cum) * step[:, span])
            pack[0:heads, :] = first
            pack[half : half + heads, :] = second
            b_packs[span] = pack[...].T.astype(BF16)
            first, second = split(jnp.exp(mid))
            g_packs[8 * block : 8 * block + 8] = turned(first, second)

    @pl.when(at < blocks - 1)
    def _():
        buf[0:HALO] = before_ref[HALO : 2 * HALO].astype(F32)

    for level in range(min(halvings, blocks - 2)):
        @pl.when(at == level + 1)
        def _():
            log_finish(level)

    last = at == blocks - 1

    @pl.when(last)
    def _():
        for level in range(min(halvings, blocks - 2), halvings):
            log_finish(level)
        halo_copy.wait()
        buf[0:HALO] = jnp.where(place == 0, 0.0, halo[HALO : 2 * HALO].astype(F32))

    block = lax.rem(at + 1, blocks)
    b_pack = b_packs[pl.ds(pl.multiple_of(block * GROUP, GROUP), GROUP)]
    g_pack = g_packs[pl.ds(pl.multiple_of(block * 8, 8), 8)].astype(BF16)

    def mix(columns):
        pieces = []
        for start in range(columns.start, columns.stop, LANES):
            lanes = slice(start, start + LANES)
            rows = jnp.concatenate([buf[0:HALO, lanes], input_ref[:, lanes].astype(F32)], axis=0)
            weights = 0.5 * weight_ref[:, lanes]
            total = rows * weights[0:1]
            for k in range(1, 4):
                total = pltpu.roll(total, 1, 0) + rows * weights[k : k + 1]
            part = total[HALO:] + 0.5 * bias_ref[lanes].reshape(1, LANES)
            pieces.append((part + part * jnp.tanh(part)).astype(BF16))
        return jnp.concatenate(pieces, axis=1)

    bc = mix(slice(inner, inner + WIDE))
    bc_ref[...] = bc
    b_turned = bc[:, : WIDE // 2].astype(F32).T.astype(BF16)

    def chunk(j):
        columns = slice(j * WIDE, (j + 1) * WIDE)
        wide = spread[:, columns]
        xb = (mix(columns).astype(F32) * dot(b_pack, wide)).astype(BF16)
        xb_ref[:, columns] = xb
        g8 = dot(g_pack, wide)
        g_ref[:, columns] = g8
        return columns, g8[0:1], dot(b_turned, xb)

    @pl.when(at < blocks - 1)
    def _():
        for j in range(inner // WIDE):
            columns, g, update = chunk(j)
            state_ref[:, columns] = g * (g * state_ref[:, columns] + update)
            wide_decay[0:8, columns] = jnp.where(at == 0, 1.0, wide_decay[0:8, columns]) * (g * g)

    group = inner // PARTS

    def part_of(part):
        return slice(part * group, (part + 1) * group)

    def rows_of(level):
        return LANES >> (level + 1)

    def decay_row(level, which, columns):
        row = 8 + 16 * level + 8 * which
        return wide_decay[row : row + 1, columns]

    def down_copy(level, part):
        return send(down_send[level].at[part], down_recv[level].at[part], down_sems.at[level, part], partners[level])

    def up_copy(level, part):
        return send(up_send[level].at[part], up_recv[level].at[part], up_sems.at[level, part], partners[level])

    def top_copy(part):
        return send(top_send.at[part], top_recv.at[part], top_sems.at[part], partners[levels - 1])

    def down_start(level, part):
        if level == halvings:
            top_send[part] = state_ref[0 : LANES >> level, part_of(part)].astype(BF16)
            top_copy(part).start()
            return
        rows, columns, right = rows_of(level), part_of(part), rights[level] == 1
        top, bottom = state_ref[0:rows, columns], state_ref[rows : 2 * rows, columns]
        down_send[level][part] = jnp.where(right, top, bottom).astype(BF16)
        down_copy(level, part).start()
        keep[level][:, columns] = jnp.where(right, bottom, top)

    def down_finish(level, part):
        rows, columns, right = rows_of(level), part_of(part), rights[level] == 1
        down_copy(level, part).wait()
        got, mine = down_recv[level][part].astype(F32), keep[level][:, columns]
        first, second = jnp.where(right, got, mine), jnp.where(right, mine, got)
        state_ref[0:rows, columns] = decay_row(level, 1, columns) * first + second
        keep[level][:, columns] = first

    def up_start(level, part):
        rows, columns, right = rows_of(level), part_of(part), rights[level] == 1
        prefix = state_ref[0:rows, columns]
        later = decay_row(level, 0, columns) * prefix + keep[level][:, columns]
        up_send[level][part] = jnp.where(right, prefix, later).astype(BF16)
        up_copy(level, part).start()
        keep[level][:, columns] = jnp.where(right, later, prefix)

    def up_finish(level, part):
        rows, columns, right = rows_of(level), part_of(part), rights[level] == 1
        up_copy(level, part).wait()
        got, mine = up_recv[level][part].astype(F32), keep[level][:, columns]
        state_ref[0:rows, columns] = jnp.where(right, got, mine)
        state_ref[rows : 2 * rows, columns] = jnp.where(right, mine, got)

    @pl.when(last)
    def _():
        decays = []
        for level in range(halvings):
            for log in (log_first[level], log_second[level]):
                first, second = split(jnp.exp(log))
                lane = lax.broadcasted_iota(jnp.int32, (8, LANES), 1)
                decays.append(jnp.where(lane < half, first, pltpu.roll(second, half, 1)))
        decay_pack = jnp.concatenate(decays, axis=0).astype(BF16)
        for j in range(inner // WIDE):
            columns, g, update = chunk(j)
            state_ref[:, columns] = state_ref[:, columns] + wide_decay[0:1, columns] * (g * update)
            wide_decay[8 : 8 + 16 * halvings, columns] = dot(decay_pack, spread[:, columns])
            for part in range(PARTS):
                if (part + 1) * group == (j + 1) * WIDE:
                    down_start(0, part)
        for level in range(halvings):
            for part in range(PARTS):
                down_finish(level, part)
                down_start(level + 1, part)
        for part in range(PARTS):
            top_copy(part).wait()
            state_ref[0 : LANES >> halvings, part_of(part)] = jnp.where(
                rights[levels - 1] == 1, top_recv[part].astype(F32), 0.0
            )
            up_start(halvings - 1, part)
        for level in reversed(range(halvings)):
            for part in range(PARTS):
                up_finish(level, part)
                if level > 0:
                    up_start(level - 1, part)


def back_kernel(
    inner, heads,
    xb_ref, bc_ref, a_ref, g_ref, incoming_ref, gain_ref,
    out_ref,
    state, rows, spread,
):
    @pl.when(pl.program_id(0) == 0)
    def _():
        state[...] = incoming_ref[...]
        fill_spread(spread, heads)

    bc = bc_ref[...]
    width = WIDE // 2
    b, c = bc[:, :width], bc[:, width:]
    b_turned = b.astype(F32).T.astype(BF16)
    scores = dot(c, b_turned)
    scores = jnp.where(lower_triangle(), scores, 0.0).astype(BF16)
    c_twice = jnp.concatenate([c, c], axis=1)
    a_pack = a_ref[...]
    squares = jnp.zeros((GROUP, WIDE), F32)
    for j in range(inner // WIDE):
        columns = slice(j * WIDE, (j + 1) * WIDE)
        xb = xb_ref[:, columns]
        g = g_ref[0:1, columns]
        held = g * state[:, columns]
        high = held.astype(BF16)
        low = (held - high.astype(F32)).astype(BF16)
        total = dot(scores, xb) + dot(c_twice, jnp.concatenate([high, low], axis=0))
        y = total * dot(a_pack, spread[:, columns])
        rows[:, columns] = y
        squares = squares + y * y
        state[:, columns] = g * (held + dot(b_turned, xb))
    mean = jnp.sum(squares, axis=1, keepdims=True) * (1.0 / inner)
    scale = lax.rsqrt(mean + 1e-05)
    for j in range(inner // WIDE):
        columns = slice(j * WIDE, (j + 1) * WIDE)
        out_ref[:, columns] = (rows[:, columns] * scale * gain_ref[columns].reshape(1, WIDE)).astype(BF16)


def per_device(conv_input, step_raw, conv_weight, conv_bias, step_bias, decay_rate, norm_gain):
    tokens, conv_dim = conv_input.shape
    heads, inner = decay_rate.shape[0], norm_gain.shape[0]
    blocks = tokens // GROUP
    count = lax.axis_size("seq")
    levels = count.bit_length() - 1
    halvings = levels - 1
    group = inner // PARTS
    sizes = [LANES >> (level + 1) for level in range(halvings)]

    def whole(*shape):
        return pl.BlockSpec(shape, lambda i: (0,) * len(shape))

    def stepped(*shape):
        return pl.BlockSpec(shape, lambda i: (i, 0))

    def turned(*shape):
        return pl.BlockSpec(shape, lambda i: (lax.rem(i + 1, blocks), 0))

    def vmem(*shape, dtype=F32):
        return pltpu.VMEM(shape, dtype)

    slots = [vmem(PARTS, rows, group, dtype=BF16) for rows in sizes]
    shape = jax.ShapeDtypeStruct
    xb, bc, a, g, state = pl.pallas_call(
        functools.partial(front_kernel, inner, heads, blocks, count),
        grid=(blocks,),
        in_specs=[
            pl.BlockSpec((16, conv_dim), lambda i: (jnp.maximum(lax.rem(i + 1, blocks) * (GROUP // 16) - 1, 0), 0)),
            turned(GROUP, conv_dim), pl.BlockSpec(memory_space=pl.ANY),
            whole(heads, tokens), whole(4, conv_dim), whole(conv_dim), whole(heads), whole(heads),
        ],
        out_specs=[
            turned(GROUP, inner), turned(GROUP, WIDE), whole(tokens, LANES), turned(8, inner),
            whole(LANES, inner),
        ],
        out_shape=[
            shape((tokens, inner), BF16), shape((tokens, WIDE), BF16), shape((tokens, LANES), BF16),
            shape((8 * blocks, inner), F32), shape((LANES, inner), F32),
        ],
        scratch_shapes=[
            vmem(HALO, conv_dim), vmem(16, conv_dim, dtype=BF16), vmem(LANES, inner, dtype=BF16),
            vmem(LANES, GROUP), vmem(LANES, LANES), vmem(tokens, LANES, dtype=BF16), vmem(8 * blocks, LANES),
            vmem(halvings, 8, LANES), vmem(halvings, 8, LANES), vmem(halvings, 8, LANES), vmem(halvings, 8, LANES),
            vmem(8 + 16 * halvings, inner),
            [vmem(rows, inner) for rows in sizes], slots, slots,
            vmem(PARTS, LANES >> halvings, group, dtype=BF16), vmem(PARTS, LANES >> halvings, group, dtype=BF16),
            slots, slots,
            pltpu.SemaphoreType.DMA((2,)), pltpu.SemaphoreType.DMA((halvings, 2)),
            pltpu.SemaphoreType.DMA((halvings, PARTS, 2)), pltpu.SemaphoreType.DMA((PARTS, 2)),
            pltpu.SemaphoreType.DMA((halvings, PARTS, 2)),
        ],
        compiler_params=pltpu.CompilerParams(collective_id=0, has_side_effects=True, vmem_limit_bytes=60 * 1024 * 1024),
        name="front",
    )(conv_input, conv_input, conv_input, step_raw.T, conv_weight, conv_bias, step_bias, decay_rate)
    return pl.pallas_call(
        functools.partial(back_kernel, inner, heads),
        grid=(blocks,),
        in_specs=[
            stepped(GROUP, inner), stepped(GROUP, WIDE), stepped(GROUP, LANES), stepped(8, inner),
            whole(LANES, inner), whole(inner),
        ],
        out_specs=stepped(GROUP, inner),
        out_shape=shape((tokens, inner), BF16),
        scratch_shapes=[vmem(LANES, inner), vmem(GROUP, inner), vmem(LANES, inner, dtype=BF16)],
        name="back",
    )(xb, bc, a, g, state, norm_gain)


def solution(mesh):
    placed = (P(("parts", "seq"), None), P(("parts", "seq"), None), P(), P(), P(), P(), P())
    return jax.shard_map(
        per_device, mesh=mesh, in_specs=placed, out_specs=P(("parts", "seq"), None), check_vma=False
    )
```
